256 devices in a mesh: grp: 16 (over y, z_hi), blk: 16 (over x, z_lo, core).
Axes of the slice: x: 4, y: 4, z: 8 (z_hi: 4, z_lo: 2; z = z_hi * 2 + z_lo), core: 2. Of those that a mesh axis runs over, the one named last changes fastest.
Arguments:
- feats: bfloat16 [196608, 128], P(('grp', 'blk')), may hold values from -6 to 6
- proj: bfloat16 [128, 512], replicated, may hold values from -0.5 to 0.5
- att_src: float32 [8, 64], replicated
- target_attention_vector: float32 [8, 64], replicated
- edge_mask: int32 [196608, 5, 768], P(('grp', 'blk')), may hold values from 0 to 1
- send_rows: int32 [256, 16, 32], P(('grp', 'blk')), may hold values from 0 to 767
- send_count: int32 [16, 16, 16], P(None, 'blk', 'grp'), may hold values from 0 to 32, as said below
- bound_mask: int32 [196608, 512], P(('grp', 'blk')), may hold values 0 or 1
Outputs:
- node_out: bfloat16 [196608, 512], P(('grp', 'blk'))
The draws below stay inside these ranges and needn't reach their ends.
Inputs may be any that keep to these rules, and one draw needn't show every extreme that they name: `send_count`: a group sends nothing to itself; every device fills all 32 slots for some other group.
All inputs are finite; a program needn't handle non-finite values. No bound on the sum of `bound_mask` on one device may be relied on, other than what follows from the above.
Results may differ from the reference program's by a relative error of at most 0.0095.
Values may be sent and summed in bfloat16 or wider, within the bound.
No kernel may reach another device: no remote copies, remote signals or barrier semaphores. Data moves between devices by JAX's collectives and lax.ppermute only.
A program may use at most 64 MiB of HBM per device.

```python
import jax
import jax.numpy as jnp
from jax import lax

F_IN = 128
HEADS = 8
HEAD_DIM = 64
WIDTH = 512
NODE_DEV = 768
TILE = 128
HOPS = 5
CAP = 32
NODES = 196608
SLOTS = 512
N_GRP = 16
N_BLK = 16


def draw_att_src(key, part):
    values = jax.random.normal(jax.random.fold_in(key, 11), (HEADS, HEAD_DIM), jnp.float32)
    return values * 0.15


def draw_target_attention_vector(key, part):
    values = jax.random.normal(jax.random.fold_in(key, 12), (HEADS, HEAD_DIM), jnp.float32)
    return values * 0.15


def draw_edge_mask(key, part):
    tile_key = jax.random.fold_in(key, 21)
    cell_key = jax.random.fold_in(key, 22)
    tiles_dst = NODES // TILE
    tiles_src = NODE_DEV // TILE
    block_pos = jnp.arange(tiles_dst, dtype=jnp.int32) * TILE // NODE_DEV % N_BLK
    density = 15 + 70 * block_pos // max(N_BLK - 1, 1)
    active = jax.random.randint(tile_key, (tiles_dst, HOPS, tiles_src), 0, 100) < density[:, None, None]
    active = jnp.repeat(jnp.repeat(active, TILE, axis=0), TILE, axis=2)
    inner = jax.random.randint(cell_key, (NODES, HOPS, NODE_DEV), 0, 100) < 30
    return (active & inner).astype(jnp.int32)


def draw_send_count(key, part):
    base_key = jax.random.fold_in(key, 31)
    pick_key = jax.random.fold_in(key, 32)
    base = jax.random.randint(base_key, (N_GRP, N_BLK, N_GRP), 0, CAP + 1)
    offset = jax.random.randint(pick_key, (N_GRP, N_BLK, 1), 1, N_GRP)
    sender = jnp.arange(N_GRP, dtype=jnp.int32)[:, None, None]
    target = jnp.arange(N_GRP, dtype=jnp.int32)[None, None, :]
    base = jnp.where(target == (sender + offset) % N_GRP, CAP, base)
    return jnp.where(target == sender, 0, base).astype(jnp.int32)


def set_ends(values, rng, low, high):
    longest = values.shape.index(max(values.shape))
    spots = []
    for shift in (0, 1):
        where = [jax.random.randint(jax.random.fold_in(rng, axis), (), 0, length) for axis, length in enumerate(values.shape)]
        where[longest] = (where[longest] + shift) % values.shape[longest]
        spots.append(tuple(where))
    return values.at[spots[0]].set(low).at[spots[1]].set(high)


def block_scale(rng, shape, pieces, low, largest):
    factor_of = 1.0
    for axis_at, blocks in pieces:
        draws = jax.random.uniform(jax.random.fold_in(jax.random.fold_in(rng, 6), axis_at), (blocks,), jnp.float32, low / len(pieces), largest / len(pieces))
        factor_of = factor_of * jnp.repeat(jnp.exp(draws), shape[axis_at] // blocks).reshape((-1,) + (1,) * (len(shape) - 1 - axis_at))
    return factor_of


def gaussian(own_key, extent, width, most, shards=(), kind=jnp.bfloat16):
    values = width * jax.random.normal(own_key, extent, jnp.float32)
    if shards:
        values = values * block_scale(own_key, extent, shards, -0.22, 0.18)
    return jnp.clip(values, -most, most).astype(kind)


def setup_inputs(seed: int = 0) -> dict:
    arg_keys = jax.random.split(jax.random.key(seed), 9)
    return {
        "feats": gaussian(arg_keys[0], (NODES, F_IN), 1.0, 6.0, ((0, 256),)),
        "proj": gaussian(arg_keys[1], (F_IN, WIDTH), F_IN ** -0.5, 0.5),
        "att_src": draw_att_src(jax.random.fold_in(arg_keys[8], 71), 0),
        "target_attention_vector": draw_target_attention_vector(jax.random.fold_in(arg_keys[8], 71), 0),
        "edge_mask": draw_edge_mask(jax.random.fold_in(arg_keys[8], 71), 0),
        "send_rows": set_ends(jax.random.randint(arg_keys[5], (NODES // NODE_DEV, N_GRP, CAP), 0, NODE_DEV), jax.random.fold_in(arg_keys[5], 1), 0, NODE_DEV - 1).astype(jnp.int32),
        "send_count": draw_send_count(jax.random.fold_in(arg_keys[8], 71), 0),
        "bound_mask": set_ends((jax.random.randint(arg_keys[7], (NODES, SLOTS), 0, 8) < 1).astype(jnp.int32), jax.random.fold_in(arg_keys[7], 1), 0, 1),
    }


def head_logits(hidden, vector):
    count = hidden.shape[0]
    reshaped_rows = hidden.astype(jnp.float32).reshape(count, HEADS, HEAD_DIM)
    return jnp.einsum("nhd,hd->nh", reshaped_rows, vector.astype(jnp.float32), precision=lax.Precision.HIGHEST)


def edge_scores(dst_score, src_score, allowed):
    raw = dst_score.T[:, :, None] + src_score.T[:, None, :]
    raw = jnp.where(raw > 0, raw, 0.2 * raw)
    return jnp.where(allowed[None, :, :], raw, -jnp.inf)


def attend(dst_score, sources, att_src):
    count = dst_score.shape[0]
    top = jnp.full((HEADS, count), -jnp.inf, jnp.float32)
    for block, allowed in sources:
        scores = edge_scores(dst_score, head_logits(block, att_src), allowed)
        top = jnp.maximum(top, jnp.max(scores, axis=2))
    total = jnp.zeros((HEADS, count), jnp.float32)
    item_number = jnp.zeros((HEADS, count, HEAD_DIM), jnp.float32)
    for block, allowed in sources:
        scores = edge_scores(dst_score, head_logits(block, att_src), allowed)
        weight_matrix = jnp.exp(scores - top[:, :, None]).astype(jnp.bfloat16)
        total = total + jnp.sum(weight_matrix.astype(jnp.float32), axis=2)
        reshaped_rows = block.astype(jnp.float32).reshape(block.shape[0], HEADS, HEAD_DIM)
        item_number = item_number + jnp.einsum("exv,vej->exj", weight_matrix.astype(jnp.float32), reshaped_rows)
    merged = item_number / total[:, :, None]
    merged = jnp.transpose(merged, (1, 0, 2)).reshape(count, HEADS * HEAD_DIM)
    return jax.nn.elu(merged).astype(jnp.bfloat16)


def reference(feats, proj, att_src, target_attention_vector, edge_mask, send_rows, send_count, bound_mask):
    hidden = jnp.dot(feats, proj, preferred_element_type=jnp.float32).astype(jnp.bfloat16)
    dst_all = head_logits(hidden, target_attention_vector)
    self_loop = jnp.eye(NODE_DEV, dtype=bool)
    slot_indices = jnp.arange(CAP, dtype=jnp.int32)

    def one_device(device):
        group = device // N_BLK
        block_id = device % N_BLK
        start = (device * NODE_DEV).astype(jnp.int32)
        dst_score = lax.dynamic_slice_in_dim(dst_all, start, NODE_DEV, 0)
        masks = lax.dynamic_slice_in_dim(edge_mask, start, NODE_DEV, 0)
        sources = []
        for hop in range(HOPS):
            peer = group * N_BLK + (block_id - hop) % N_BLK
            rows = lax.dynamic_slice_in_dim(hidden, (peer * NODE_DEV).astype(jnp.int32), NODE_DEV, 0)
            allowed = masks[:, hop, :] > 0
            if hop == 0:
                allowed = allowed | self_loop
            sources.append((rows, allowed))
        peers = jnp.arange(N_GRP, dtype=jnp.int32) * N_BLK + block_id
        picked = send_rows[peers, group, :]
        global_rows = (peers[:, None] * NODE_DEV + picked).reshape(-1).astype(jnp.int32)
        slots = hidden[global_rows]
        counts = send_count[:, block_id, group]
        live = (slot_indices[None, :] < counts[:, None]).reshape(-1)
        bound = lax.dynamic_slice_in_dim(bound_mask, start, NODE_DEV, 0) > 0
        sources.append((slots, bound & live[None, :]))
        return attend(dst_score, sources, att_src)

    result = lax.map(one_device, jnp.arange(N_GRP * N_BLK, dtype=jnp.int32))
    return result.reshape(NODES, HEADS * HEAD_DIM)
```

```python
import functools

import jax
import jax.numpy as jnp
from jax import lax
from jax.experimental import pallas as pl
from jax.experimental.pallas import tpu as pltpu
from jax.sharding import PartitionSpec as P

HEADS = 8
HEAD_DIM = 64
HOPS = 5
ROWS = 80
TILE = 256
SPAN = 60.0
F32 = jnp.float32
BF16 = jnp.bfloat16
NT = (((1,), (1,)), ((), ()))
NN = (((1,), (0,)), ((), ()))


def mm(a, b, dims):
    return lax.dot_general(a, b, dims, preferred_element_type=F32)


def pieces(x):
    hi = x.astype(BF16)
    rest = x - hi.astype(F32)
    mid = rest.astype(BF16)
    low = (rest - mid.astype(F32)).astype(BF16)
    return hi, mid, low


def pick_kernel(rows_ref, feats_ref, out_ref, chosen):
    groups, cap = rows_ref.shape
    count = feats_ref.shape[0]
    rows = rows_ref[...].astype(F32)
    high = jnp.floor(rows * (1.0 / 256.0))
    low = rows - 256.0 * high
    unit = (
        lax.broadcasted_iota(jnp.int32, (cap, cap), 0) == lax.broadcasted_iota(jnp.int32, (cap, cap), 1)
    ).astype(F32).astype(BF16)
    turned = mm(unit, high.astype(BF16), NT) * 256.0 + mm(unit, low.astype(BF16), NT)
    turned = turned.astype(jnp.int32)
    lane = lax.broadcasted_iota(jnp.int32, (cap, count), 1)
    for p in range(groups):
        hit = lane == turned[:, p : p + 1]
        chosen[p * cap : (p + 1) * cap, :] = jnp.where(hit, 1.0, 0.0).astype(BF16)
    out_ref[...] = mm(chosen[...], feats_ref[...], NN).astype(BF16)


def pick_rows(send_rows, feats):
    groups, cap = send_rows.shape
    return pl.pallas_call(
        pick_kernel,
        out_shape=jax.ShapeDtypeStruct((groups * cap, feats.shape[1]), BF16),
        scratch_shapes=[pltpu.VMEM((groups * cap, feats.shape[0]), BF16)],
        name="pick_rows",
    )(send_rows, feats)


def spread_heads(vector):
    width = HEADS * HEAD_DIM
    tiler = (
        lax.broadcasted_iota(jnp.int32, (HEAD_DIM, width), 1) % HEAD_DIM
        == lax.broadcasted_iota(jnp.int32, (HEAD_DIM, width), 0)
    )
    tiler = jnp.where(tiler, 1.0, 0.0).astype(BF16)
    own = (
        lax.broadcasted_iota(jnp.int32, (HEADS, width), 1) // HEAD_DIM
        == lax.broadcasted_iota(jnp.int32, (HEADS, width), 0)
    )
    parts = [jnp.where(own, mm(p, tiler, NN), 0.0) for p in pieces(vector)]
    parts.append(jnp.zeros((HEADS, width), F32))
    return jnp.concatenate(parts, axis=0).astype(BF16)


def logits(spread, turned):
    s = mm(spread, turned, NN)
    return s[0:HEADS] + s[HEADS : 2 * HEADS] + s[2 * HEADS : 3 * HEADS]


def elu(x):
    small = x * (1.0 + 0.5 * x)
    low = jnp.where(x > -1e-3, small, jnp.exp(jnp.minimum(x, 0.0)) - 1.0)
    return jnp.where(x > 0, x, low)


def attend_kernel(
    count_ref, x0, x1, x2, x3, x4, xs, proj_ref, src_ref, dst_ref, edge_ref, bound_ref,
    out_ref,
    table, up, down, ratio, score, dcol, mask, turned_out, wide,
):
    step = pl.program_id(0)
    tile = out_ref.shape[0]
    nodes = x0.shape[0]
    slots = xs.shape[0]
    cap = slots // count_ref.shape[0]
    sources = HOPS * nodes + slots
    spans = [(b * nodes, nodes) for b in range(HOPS)] + [(HOPS * nodes, slots)]

    @pl.when(step == 0)
    def _():
        proj_t = proj_ref[...].T
        spread_src = spread_heads(src_ref[...])
        spread_dst = spread_heads(dst_ref[...])
        worst = jnp.zeros((HEADS, 1), F32)
        for b, (x, (start, size)) in enumerate(zip((x0, x1, x2, x3, x4, xs), spans)):
            turned = mm(proj_t, x[...], NT).astype(BF16)
            for h in range(HEADS):
                table[h, 0:HEAD_DIM, start : start + size] = turned[h * HEAD_DIM : (h + 1) * HEAD_DIM]
            s = logits(spread_src, turned)
            score[:, start : start + size] = s
            worst = jnp.maximum(worst, jnp.max(jnp.abs(s), axis=1, keepdims=True))
            rise, slow = jnp.exp(s), jnp.exp(0.2 * s)
            for h in range(HEADS):
                up[h, :, start : start + size] = jnp.broadcast_to(rise[h : h + 1], (16, size)).astype(BF16)
                down[h, :, start : start + size] = jnp.broadcast_to(slow[h : h + 1], (16, size)).astype(BF16)
            if b == 0:
                d = logits(spread_dst, turned)
                worst = jnp.maximum(worst, jnp.max(jnp.abs(d), axis=1, keepdims=True))
                d_cols = d.T
                dcol[...] = d_cols
                r_cols = jnp.exp(-0.8 * d_cols)
                for h in range(HEADS):
                    ratio[h] = jnp.broadcast_to(r_cols[:, h : h + 1], (nodes, 128)).astype(BF16)
        for h in range(HEADS):
            table[h, HEAD_DIM:ROWS, :] = jnp.ones((ROWS - HEAD_DIM, sources), BF16)
        wide[0] = (jnp.max(worst) > SPAN).astype(jnp.int32)

    lane = lax.broadcasted_iota(jnp.int32, (1, slots), 1)
    live = jnp.zeros((1, slots), F32)
    for p in range(count_ref.shape[0]):
        live = jnp.where((lane // cap == p) & (lane % cap < count_ref[p]), 1.0, live)
    for b, (start, size) in enumerate(spans):
        m = (bound_ref[...] if b == HOPS else edge_ref[b]).astype(F32)
        if b == 0:
            row = lax.broadcasted_iota(jnp.int32, (tile, size), 0) + step * tile
            m = jnp.where(row == lax.broadcasted_iota(jnp.int32, (tile, size), 1), 1.0, m)
        if b == HOPS:
            m = m * live
        mask[:, start : start + size] = m.astype(BF16)

    @pl.when(wide[0] == 0)
    def _():
        for h in range(HEADS):
            r = ratio[h, pl.ds(pl.multiple_of(step * tile, tile), tile), :].reshape(tile // 16, 16, 128)
            acc = jnp.zeros((ROWS, tile), F32)
            for start, size in spans:
                reach = pl.ds(start, size)
                r_all = jnp.concatenate([r] * (size // 128), axis=2)
                w = jnp.maximum(up[h, :, reach][None], r_all * down[h, :, reach][None])
                w = w.reshape(tile, size) * mask[:, reach]
                acc += mm(table[h, :, reach], w, NT)
            o = acc[0:HEAD_DIM] * (1.0 / acc[HEAD_DIM : HEAD_DIM + 1])
            turned_out[h * HEAD_DIM : (h + 1) * HEAD_DIM, :] = elu(o)
        out_ref[...] = turned_out[...].T.astype(BF16)

    @pl.when(wide[0] != 0)
    def _():
        def one_head(h, carry):
            d_tile = dcol[pl.ds(pl.multiple_of(step * tile, tile), tile), :]
            column = lax.broadcasted_iota(jnp.int32, d_tile.shape, 1)
            d = jnp.sum(jnp.where(column == h, d_tile, 0.0), axis=1, keepdims=True)

            def scores(start, size):
                v = d + score[pl.ds(h, 1), pl.ds(start, size)]
                v = jnp.maximum(v, 0.2 * v)
                return jnp.where(mask[:, pl.ds(start, size)].astype(F32) > 0, v, -jnp.inf)

            top = jnp.full((tile, 1), -jnp.inf, F32)
            for start, size in spans:
                top = jnp.maximum(top, jnp.max(scores(start, size), axis=1, keepdims=True))
            acc = jnp.zeros((ROWS, tile), F32)
            for start, size in spans:
                w = jnp.exp(scores(start, size) - top).astype(BF16)
                acc += mm(table[h, :, pl.ds(start, size)], w, NT)
            o = acc[0:HEAD_DIM] * (1.0 / acc[HEAD_DIM : HEAD_DIM + 1])
            turned_out[pl.ds(pl.multiple_of(h * HEAD_DIM, HEAD_DIM), HEAD_DIM), :] = elu(o)
            return carry

        lax.fori_loop(0, HEADS, one_head, 0)
        out_ref[...] = turned_out[...].T.astype(BF16)


def attend(counts, blocks, slots, proj, att_src, att_dst, edges, bound, interpret=False):
    nodes = blocks[0].shape[0]
    n_slots = slots.shape[0]
    sources = HOPS * nodes + n_slots
    width = proj.shape[1]
    whole = pl.BlockSpec(memory_space=pltpu.VMEM)
    return pl.pallas_call(
        attend_kernel,
        grid=(nodes // TILE,),
        out_shape=jax.ShapeDtypeStruct((nodes, width), BF16),
        in_specs=[pl.BlockSpec(memory_space=pltpu.SMEM)]
        + [whole] * 9
        + [
            pl.BlockSpec((HOPS, TILE, nodes), lambda i: (0, i, 0)),
            pl.BlockSpec((TILE, n_slots), lambda i: (i, 0)),
        ],
        out_specs=pl.BlockSpec((TILE, width), lambda i: (i, 0)),
        scratch_shapes=[
            pltpu.VMEM((HEADS, ROWS, sources), BF16),
            pltpu.VMEM((HEADS, 16, sources), BF16),
            pltpu.VMEM((HEADS, 16, sources), BF16),
            pltpu.VMEM((HEADS, nodes, 128), BF16),
            pltpu.VMEM((HEADS, sources), F32),
            pltpu.VMEM((nodes, HEADS), F32),
            pltpu.VMEM((TILE, sources), BF16),
            pltpu.VMEM((width, TILE), F32),
            pltpu.SMEM((1,), jnp.int32),
        ],
        compiler_params=pltpu.CompilerParams(vmem_limit_bytes=56 << 20),
        interpret=interpret,
        name="attend",
    )(counts, *blocks, slots, proj, att_src, att_dst, edges, bound)


def passed_along(block, axis, distance):
    devices = range(lax.axis_size(axis))
    return lax.ppermute(block, axis, [((i - distance) % len(devices), i) for i in devices])


def other_core(block):
    return lax.ppermute(block, "blk", [(i, i ^ 1) for i in range(lax.axis_size("blk"))])


def local(feats, proj, att_src, att_dst, edge_mask, send_rows, send_count, bound_mask):
    outgoing = pick_rows(send_rows[0], feats)
    two = passed_along(feats, "blk", 2)
    four = passed_along(feats, "blk", 4)
    arrived = lax.all_to_all(outgoing, "grp", split_axis=0, concat_axis=0, tiled=True)
    second = lax.axis_index("blk") % 2 == 1
    outer = other_core(jnp.where(second, four, feats))
    inner = other_core(two)
    one = jnp.where(second, outer, inner)
    three = jnp.where(second, inner, outer)
    edges = jnp.transpose(edge_mask, (1, 0, 2))
    return attend(
        send_count.reshape(-1), (feats, one, two, three, four), arrived, proj, att_src, att_dst, edges, bound_mask
    )


def solution(mesh):
    in_specs = (
        P(("grp", "blk"), None),
        P(),
        P(),
        P(),
        P(("grp", "blk"), None, None),
        P(("grp", "blk"), None, None),
        P(None, "blk", "grp"),
        P(("grp", "blk"), None),
    )
    out_specs = P(("grp", "blk"), None)
    return jax.shard_map(local, mesh=mesh, in_specs=in_specs, out_specs=out_specs, check_vma=False)
```

```python
import functools

import jax
import jax.numpy as jnp
from jax import lax
from jax.experimental import pallas as pl
from jax.experimental.pallas import tpu as pltpu
from jax.sharding import PartitionSpec as P

HEADS = 8
HEAD_DIM = 64
HOPS = 5
LANES = 128
ROWS = 80
TILE = 256
SPAN = 60.0
F32 = jnp.float32
BF16 = jnp.bfloat16
NT = (((1,), (1,)), ((), ()))
NN = (((1,), (0,)), ((), ()))
WHOLE = pl.BlockSpec(memory_space=pltpu.VMEM)


def mm(a, b, dims=NN):
    return lax.dot_general(a, b, dims, preferred_element_type=F32)


def in_hbm(x):
    return pltpu.with_memory_space_constraint(x, pltpu.HBM)


def iota(shape, axis):
    return lax.broadcasted_iota(jnp.int32, shape, axis)


def pieces(x):
    hi = x.astype(BF16)
    rest = x - hi.astype(F32)
    mid = rest.astype(BF16)
    low = (rest - mid.astype(F32)).astype(BF16)
    return hi, mid, low


def pick_kernel(rows_ref, feats_ref, out_ref, chosen):
    groups, cap = rows_ref.shape
    count = feats_ref.shape[0]
    rows = rows_ref[...].astype(F32)
    high = jnp.floor(rows * (1.0 / 256.0))
    low = rows - 256.0 * high
    unit = jnp.where(iota((cap, cap), 0) == iota((cap, cap), 1), 1.0, 0.0).astype(BF16)
    turned = mm(unit, high.astype(BF16), NT) * 256.0 + mm(unit, low.astype(BF16), NT)
    turned = turned.astype(jnp.int32)
    lane = iota((cap, count), 1)
    for p in range(groups):
        hit = lane == turned[:, p : p + 1]
        chosen[p * cap : (p + 1) * cap, :] = jnp.where(hit, 1.0, 0.0).astype(BF16)
    out_ref[...] = mm(chosen[...], feats_ref[...]).astype(BF16)


def pick_rows(send_rows, feats):
    groups, cap = send_rows.shape
    return pl.pallas_call(
        pick_kernel,
        out_shape=jax.ShapeDtypeStruct((groups * cap, feats.shape[1]), BF16),
        scratch_shapes=[pltpu.VMEM((groups * cap, feats.shape[0]), BF16)],
        name="pick_rows",
    )(send_rows, feats)


def spread_heads(vector):
    width = HEADS * HEAD_DIM
    tiler = jnp.where(iota((HEAD_DIM, width), 1) % HEAD_DIM == iota((HEAD_DIM, width), 0), 1.0, 0.0).astype(BF16)
    own = iota((HEADS, width), 1) // HEAD_DIM == iota((HEADS, width), 0)
    parts = [jnp.where(own, mm(p, tiler), 0.0) for p in pieces(vector)]
    parts.append(jnp.zeros((HEADS, width), F32))
    return jnp.concatenate(parts, axis=0).astype(BF16)


def logits(spread, turned):
    s = mm(spread, turned)
    return s[0:HEADS] + s[HEADS : 2 * HEADS] + s[2 * HEADS : 3 * HEADS]


def steps(s):
    return jnp.exp(0.2 * s), jnp.exp(0.8 * s).T.astype(BF16)


def prepare(h, turned, flat, steep, table, rise):
    size = flat.shape[1]
    tail = jnp.broadcast_to(flat[h : h + 1], (ROWS - HEAD_DIM, size)).astype(BF16)
    part = turned[h * HEAD_DIM : (h + 1) * HEAD_DIM].reshape(HEAD_DIM // 16, 16, size) * tail[None]
    part = part.reshape(HEAD_DIM, size)
    for t in range(size // LANES):
        lanes = slice(t * LANES, (t + 1) * LANES)
        table[h, t, 0:HEAD_DIM, :] = part[:, lanes]
        table[h, t, HEAD_DIM:ROWS, :] = tail[:, lanes]
    rise[h] = jnp.broadcast_to(steep[:, h : h + 1], (size, LANES))


def weighted(h, planes, table, rise, ratio, mask):
    size = rise.shape[1]
    steep = rise[h].reshape(size // 16, 16, LANES)
    left = jnp.concatenate([table[h, t] for t in range(size // LANES)], axis=1)
    cols = []
    for plane in planes:
        w = jnp.maximum(steep, ratio[h, plane][None]) * mask[plane].reshape(size // 16, 16, LANES)
        cols.append(w.reshape(size, LANES))
    return mm(left, jnp.concatenate(cols, axis=1))


def elu(x):
    small = x * (1.0 + 0.5 * x)
    low = jnp.where(x > -1e-3, small, jnp.exp(jnp.minimum(x, 0.0)) - 1.0)
    return jnp.where(x > 0, x, low)


def largest(*scores):
    worst = functools.reduce(jnp.maximum, [jnp.max(jnp.abs(s), axis=1, keepdims=True) for s in scores])
    return jnp.broadcast_to(worst, (HEADS, LANES))


def turned_tile(m, diagonal):
    m = m.astype(F32)
    if diagonal is not None:
        m = jnp.where(iota(m.shape, 0) == iota(m.shape, 1) + diagonal, 1.0, m)
    return m.astype(BF16).T


def turn_kernel(count_ref, edge_hbm, bound_hbm, edge_out, bound_out, edge, bound, edge_t, bound_t, sems, sent):
    nodes, slots = bound.shape
    hops = edge.shape[0]
    half = nodes // 2
    planes = nodes // LANES
    cap = slots // count_ref.shape[0]
    parts = [(hop, i) for hop in range(hops) for i in range(2)]
    copies, sends = [], []
    for k, (hop, i) in enumerate(parts):
        rows, some = pl.ds(i * half, half), pl.ds(i * planes // 2, planes // 2)
        copies.append(pltpu.make_async_copy(edge_hbm.at[hop, rows, :], edge.at[hop, rows, :], sems.at[k]))
        sends.append(pltpu.make_async_copy(edge_t.at[hop, some], edge_out.at[hop, some], sent.at[k]))
    copies.append(pltpu.make_async_copy(bound_hbm, bound, sems.at[2 * hops]))
    sends.append(pltpu.make_async_copy(bound_t, bound_out, sent.at[2 * hops]))
    for copy in copies:
        copy.start()
    lane = iota((1, slots), 1)
    live = jnp.zeros((1, slots), F32)
    for p in range(count_ref.shape[0]):
        live = jnp.where((lane // cap == p) & (lane % cap < count_ref[p]), 1.0, live)
    for k, (hop, i) in enumerate(parts):
        copies[k].wait()
        for plane in range(i * planes // 2, (i + 1) * planes // 2):
            rows = slice(plane * LANES, (plane + 1) * LANES)
            for t in range(planes):
                lanes = slice(t * LANES, (t + 1) * LANES)
                edge_t[hop, plane, lanes, :] = turned_tile(edge[hop, rows, lanes], 0 if hop == 0 and t == plane else None)
        sends[k].start()
    copies[2 * hops].wait()
    for plane in range(planes):
        m = bound[plane * LANES : (plane + 1) * LANES, :].astype(F32) * live
        for t in range(slots // LANES):
            lanes = slice(t * LANES, (t + 1) * LANES)
            bound_t[plane, lanes, :] = turned_tile(m[:, lanes], None)
    sends[2 * hops].start()
    for send in sends:
        send.wait()


def turn_masks(counts, edges, bound):
    hops, nodes = edges.shape[0], edges.shape[1]
    slots = bound.shape[1]
    planes = nodes // LANES
    far = pl.BlockSpec(memory_space=pl.ANY)
    edge_t, bound_t = pl.pallas_call(
        turn_kernel,
        out_shape=(
            jax.ShapeDtypeStruct((hops, planes, nodes, LANES), BF16),
            jax.ShapeDtypeStruct((planes, slots, LANES), BF16),
        ),
        in_specs=[pl.BlockSpec(memory_space=pltpu.SMEM), far, far],
        out_specs=(pl.BlockSpec(memory_space=pltpu.HBM),) * 2,
        scratch_shapes=[
            pltpu.VMEM((hops, nodes, nodes), jnp.int32),
            pltpu.VMEM((nodes, slots), jnp.int32),
            pltpu.VMEM((hops, planes, nodes, LANES), BF16),
            pltpu.VMEM((planes, slots, LANES), BF16),
            pltpu.SemaphoreType.DMA((2 * hops + 1,)),
            pltpu.SemaphoreType.DMA((2 * hops + 1,)),
        ],
        compiler_params=pltpu.CompilerParams(vmem_limit_bytes=58 << 20),
        name="turn_masks",
    )(counts, in_hbm(edges), in_hbm(bound))
    return in_hbm(edge_t), in_hbm(bound_t)


def scratch(size, nodes, copies):
    planes = nodes // LANES
    return (
        *[pltpu.VMEM((HEADS, size // LANES, ROWS, LANES), BF16)] * copies,
        *[pltpu.VMEM((HEADS, size, LANES), BF16)] * copies,
        *[pltpu.VMEM((planes, size, LANES), BF16)] * copies,
        pltpu.VMEM((HEADS, planes, 16, LANES), BF16),
    )


def spread_ratio(d, ratio):
    r = jnp.exp(-0.8 * d)
    for h in range(HEADS):
        for p in range(d.shape[1] // LANES):
            row = r[h : h + 1, p * LANES : (p + 1) * LANES]
            ratio[h, p] = jnp.broadcast_to(row, (16, LANES)).astype(BF16)


def blocks_kernel(
    x0, x1, x2, x3, x4, proj_ref, src_ref, dst_ref, mask_hbm, acc_ref, dst_out, worst_ref, landed, sems
):
    nodes = x0.shape[0]
    planes = nodes // LANES
    per = TILE // LANES
    xs = (x0, x1, x2, x3, x4)
    copies = [pltpu.make_async_copy(mask_hbm.at[b], landed.at[b], sems.at[b]) for b in range(HOPS)]
    for copy in copies:
        copy.start()

    def body(table_a, table_b, rise_a, rise_b, mask_a, mask_b, ratio):
        tables, rises, masks = (table_a, table_b), (rise_a, rise_b), (mask_a, mask_b)
        proj_t = proj_ref[...].T
        spread = spread_heads(src_ref[...])

        def begin(b):
            turned = mm(proj_t, xs[b][...], NT).astype(BF16)
            return turned, logits(spread, turned)

        turned, s = begin(0)
        d = logits(spread_heads(dst_ref[...]), turned)
        dst_out[...] = d
        spread_ratio(d, ratio)
        worst = largest(s, d)
        flat, steep = steps(s)
        for h in range(HEADS):
            prepare(h, turned, flat, steep, table_a, rise_a)
        copies[0].wait()
        for p in range(planes):
            mask_a[p] = landed[0, p]
        for b in range(HOPS):
            now, later = b % 2, (b + 1) % 2
            if b + 1 < HOPS:
                turned, s = begin(b + 1)
                worst = jnp.maximum(worst, largest(s))
                flat, steep = steps(s)
                copies[b + 1].wait()
                for p in range(planes):
                    masks[later][p] = landed[b + 1, p]
            for h in range(HEADS):
                if b + 1 < HOPS:
                    prepare(h, turned, flat, steep, tables[later], rises[later])
                for i in range(nodes // TILE):
                    lanes = slice(i * TILE, (i + 1) * TILE)
                    part = weighted(h, range(i * per, (i + 1) * per), tables[now], rises[now], ratio, masks[now])
                    acc_ref[h, :, lanes] = part if b == 0 else acc_ref[h, :, lanes] + part
        worst_ref[...] = worst

    pl.run_scoped(body, *scratch(nodes, nodes, 2))


def node_blocks(blocks, proj, att_src, att_dst, mask):
    nodes = blocks[0].shape[0]
    shape = jax.ShapeDtypeStruct
    return pl.pallas_call(
        blocks_kernel,
        out_shape=(shape((HEADS, ROWS, nodes), F32), shape((HEADS, nodes), F32), shape((HEADS, LANES), F32)),
        in_specs=[WHOLE] * 8 + [pl.BlockSpec(memory_space=pl.ANY)],
        out_specs=(WHOLE,) * 3,
        scratch_shapes=[pltpu.VMEM(mask.shape, BF16), pltpu.SemaphoreType.DMA((HOPS,))],
        compiler_params=pltpu.CompilerParams(vmem_limit_bytes=28 << 20),
        name="node_blocks",
    )(*blocks, proj, att_src, att_dst, mask)


def last_kernel(
    x0, x1, x2, x3, x4, xs, proj_ref, src_ref, dst_ref, worst_a, acc_in, slot_hbm, edge_any,
    out_ref,
    mask_ref, sem, turned_out, raw, hidden, cols, masks, tops, sums,
):
    nodes = x0.shape[0]
    planes = nodes // LANES
    per = TILE // LANES
    arrival = pltpu.make_async_copy(slot_hbm, mask_ref, sem)
    arrival.start()
    turned_slots = mm(proj_ref[...].T, xs[...], NT).astype(BF16)
    slot_scores = logits(spread_heads(src_ref[...]), turned_slots)
    worst = jnp.max(jnp.maximum(worst_a[...], largest(slot_scores)))
    arrival.wait()

    def finish(h, acc):
        o = acc[0:HEAD_DIM] * (1.0 / acc[HEAD_DIM : HEAD_DIM + 1])
        turned_out[h * HEAD_DIM : (h + 1) * HEAD_DIM, :] = elu(o)

    @pl.when(worst <= SPAN)
    def _():
        def body(table, rise, mask, ratio):
            spread_ratio(dst_ref[...], ratio)
            flat, steep = steps(slot_scores)
            for p in range(planes):
                mask[p] = mask_ref[p]
            for h in range(HEADS):
                prepare(h, turned_slots, flat, steep, table, rise)
            for i in range(nodes // TILE):
                lanes = slice(i * TILE, (i + 1) * TILE)
                for h in range(HEADS):
                    part = weighted(h, range(i * per, (i + 1) * per), table, rise, ratio, mask)
                    finish(h, acc_in[h, :, lanes] + part)
                out_ref[lanes, :] = turned_out[...].T.astype(BF16)

        pl.run_scoped(body, *scratch(xs.shape[0], nodes, 1))

    @pl.when(jnp.logical_not(worst <= SPAN))
    def _():
        tops[...] = jnp.full(tops.shape, -jnp.inf, F32)
        sums[...] = jnp.zeros(sums.shape, F32)
        for second in (False, True):
            for b, x in enumerate((x0, x1, x2, x3, x4, xs)):
                size = x.shape[0]
                if b == HOPS:
                    masks[:, 0:size, :] = mask_ref[...]
                else:

                    def turn(p, carry):
                        pltpu.sync_copy(edge_any.at[b, pl.ds(pl.multiple_of(p * LANES, LANES), LANES), :], raw)
                        for t in range(planes):
                            lanes = slice(t * LANES, (t + 1) * LANES)
                            diagonal = (t - p) * LANES if b == 0 else None
                            masks[p, lanes, :] = turned_tile(raw[:, lanes], diagonal)
                        return carry

                    lax.fori_loop(0, planes, turn, 0)
                turned = mm(proj_ref[...].T, x[...], NT).astype(BF16)
                cols[0:size] = logits(spread_heads(src_ref[...]), turned).T
                for h in range(HEADS):
                    hidden[h, 0:HEAD_DIM, 0:size] = turned[h * HEAD_DIM : (h + 1) * HEAD_DIM]
                    hidden[h, HEAD_DIM:ROWS, 0:size] = jnp.ones((ROWS - HEAD_DIM, size), BF16)

                def one(i, carry):
                    h, p = i // planes, i % planes
                    lanes = pl.ds(pl.multiple_of(p * LANES, LANES), LANES)
                    c = cols[0:size]
                    s = jnp.sum(jnp.where(iota(c.shape, 1) == h, c, 0.0), axis=1, keepdims=True)
                    d = dst_ref[:, lanes]
                    v = s + jnp.sum(jnp.where(iota(d.shape, 0) == h, d, 0.0), axis=0, keepdims=True)
                    v = jnp.maximum(v, 0.2 * v)
                    v = jnp.where(masks[p, 0:size].astype(F32) > 0, v, -jnp.inf)
                    if second:
                        w = jnp.exp(v - tops[h, 0:1, lanes]).astype(BF16)
                        sums[h, :, lanes] += mm(hidden[h, :, 0:size], w)
                    else:
                        tops[h, :, lanes] = jnp.maximum(tops[h, :, lanes], jnp.max(v, axis=0, keepdims=True))
                    return carry

                lax.fori_loop(0, HEADS * planes, one, 0)
        for i in range(nodes // TILE):
            lanes = slice(i * TILE, (i + 1) * TILE)
            for h in range(HEADS):
                finish(h, sums[h, :, lanes])
            out_ref[lanes, :] = turned_out[...].T.astype(BF16)


def last_block(blocks, slots, proj, att_src, dst, worst, acc, bound, edges):
    nodes = acc.shape[2]
    width = proj.shape[1]
    return pl.pallas_call(
        last_kernel,
        out_shape=jax.ShapeDtypeStruct((nodes, width), BF16),
        in_specs=[WHOLE] * 11 + [pl.BlockSpec(memory_space=pl.ANY)] * 2,
        out_specs=WHOLE,
        scratch_shapes=[
            pltpu.VMEM(bound.shape, BF16),
            pltpu.SemaphoreType.DMA,
            pltpu.VMEM((width, TILE), F32),
            pltpu.VMEM((LANES, nodes), jnp.int32),
            pltpu.VMEM((HEADS, ROWS, nodes), BF16),
            pltpu.VMEM((nodes, HEADS), F32),
            pltpu.VMEM((nodes // LANES, nodes, LANES), BF16),
            pltpu.VMEM((HEADS, 8, nodes), F32),
            pltpu.VMEM((HEADS, ROWS, nodes), F32),
        ],
        compiler_params=pltpu.CompilerParams(vmem_limit_bytes=24 << 20),
        name="last_block",
    )(*blocks, slots, proj, att_src, dst, worst, acc, bound, edges)


def attend(counts, blocks, slots, proj, att_src, att_dst, edges, bound):
    mask, bound = turn_masks(counts, edges, bound)
    acc, dst, worst = node_blocks(blocks, proj, att_src, att_dst, mask)
    return last_block(blocks, slots, proj, att_src, dst, worst, acc, bound, in_hbm(edges))


def passed_along(block, axis, distance):
    devices = range(lax.axis_size(axis))
    return lax.ppermute(block, axis, [((i - distance) % len(devices), i) for i in devices])


def other_core(block):
    return lax.ppermute(block, "blk", [(i, i ^ 1) for i in range(lax.axis_size("blk"))])


def local(feats, proj, att_src, att_dst, edge_mask, send_rows, send_count, bound_mask):
    edges = in_hbm(jnp.transpose(edge_mask, (1, 0, 2)))
    two = passed_along(feats, "blk", 2)
    four = passed_along(feats, "blk", 4)
    outgoing = pick_rows(send_rows[0], feats)
    arrived = lax.all_to_all(outgoing, "grp", split_axis=0, concat_axis=0, tiled=True)
    mask, bound = turn_masks(in_hbm(send_count.reshape(-1)), edges, bound_mask)
    two, four, mask, _ = lax.optimization_barrier((two, four, mask, outgoing))
    mask = in_hbm(mask)
    second = lax.axis_index("blk") % 2 == 1
    outer = other_core(jnp.where(second, four, feats))
    inner = other_core(two)
    one = jnp.where(second, outer, inner)
    three = jnp.where(second, inner, outer)
    blocks = (feats, one, two, three, four)
    acc, dst, worst = node_blocks(blocks, proj, att_src, att_dst, mask)
    return last_block(blocks, arrived, proj, att_src, dst, worst, acc, bound, edges)


def solution(mesh):
    in_specs = (
        P(("grp", "blk"), None),
        P(),
        P(),
        P(),
        P(("grp", "blk"), None, None),
        P(("grp", "blk"), None, None),
        P(None, "blk", "grp"),
        P(("grp", "blk"), None),
    )
    out_specs = P(("grp", "blk"), None)
    return jax.shard_map(local, mesh=mesh, in_specs=in_specs, out_specs=out_specs, check_vma=False)
```

```python
import functools

import jax
import jax.numpy as jnp
from jax import lax
from jax.experimental import pallas as pl
from jax.experimental.pallas import tpu as pltpu
from jax.sharding import PartitionSpec as P

HEADS = 8
HEAD_DIM = 64
HOPS = 5
LANES = 128
ROWS = 80
TILE = 256
EARLY = 3
SPAN = 60.0
F32 = jnp.float32
BF16 = jnp.bfloat16
NT = (((1,), (1,)), ((), ()))
NN = (((1,), (0,)), ((), ()))
WHOLE = pl.BlockSpec(memory_space=pltpu.VMEM)


def mm(a, b, dims=NN):
    return lax.dot_general(a, b, dims, preferred_element_type=F32)


def in_hbm(x):
    return pltpu.with_memory_space_constraint(x, pltpu.HBM)


def iota(shape, axis):
    return lax.broadcasted_iota(jnp.int32, shape, axis)


def pieces(x):
    hi = x.astype(BF16)
    rest = x - hi.astype(F32)
    mid = rest.astype(BF16)
    low = (rest - mid.astype(F32)).astype(BF16)
    return hi, mid, low


def pick_kernel(rows_ref, feats_ref, out_ref, chosen):
    groups, cap = rows_ref.shape
    count = feats_ref.shape[0]
    rows = rows_ref[...].astype(F32)
    high = jnp.floor(rows * (1.0 / 256.0))
    low = rows - 256.0 * high
    unit = jnp.where(iota((cap, cap), 0) == iota((cap, cap), 1), 1.0, 0.0).astype(BF16)
    turned = mm(unit, high.astype(BF16), NT) * 256.0 + mm(unit, low.astype(BF16), NT)
    turned = turned.astype(jnp.int32)
    lane = iota((cap, count), 1)
    for p in range(groups):
        hit = lane == turned[:, p : p + 1]
        chosen[p * cap : (p + 1) * cap, :] = jnp.where(hit, 1.0, 0.0).astype(BF16)
    out_ref[...] = mm(chosen[...], feats_ref[...]).astype(BF16)


def pick_rows(send_rows, feats):
    groups, cap = send_rows.shape
    return pl.pallas_call(
        pick_kernel,
        out_shape=jax.ShapeDtypeStruct((groups * cap, feats.shape[1]), BF16),
        scratch_shapes=[pltpu.VMEM((groups * cap, feats.shape[0]), BF16)],
        name="pick_rows",
    )(send_rows, feats)


def spread_heads(vector):
    width = HEADS * HEAD_DIM
    tiler = jnp.where(iota((HEAD_DIM, width), 1) % HEAD_DIM == iota((HEAD_DIM, width), 0), 1.0, 0.0).astype(BF16)
    own = iota((HEADS, width), 1) // HEAD_DIM == iota((HEADS, width), 0)
    parts = [jnp.where(own, mm(p, tiler), 0.0) for p in pieces(vector)]
    parts.append(jnp.zeros((HEADS, width), F32))
    return jnp.concatenate(parts, axis=0).astype(BF16)


def logits(spread, turned):
    s = mm(spread, turned)
    return s[0:HEADS] + s[HEADS : 2 * HEADS] + s[2 * HEADS : 3 * HEADS]


def steps(s):
    return jnp.exp(0.2 * s), jnp.exp(0.8 * s).T.astype(BF16)


def prepare(h, turned, flat, steep, table, rise):
    size = flat.shape[1]
    tail = jnp.broadcast_to(flat[h : h + 1], (ROWS - HEAD_DIM, size)).astype(BF16)
    part = turned[h * HEAD_DIM : (h + 1) * HEAD_DIM].reshape(HEAD_DIM // 16, 16, size) * tail[None]
    part = part.reshape(HEAD_DIM, size)
    for t in range(size // LANES):
        lanes = slice(t * LANES, (t + 1) * LANES)
        table[h, t, 0:HEAD_DIM, :] = part[:, lanes]
        table[h, t, HEAD_DIM:ROWS, :] = tail[:, lanes]
    rise[h] = jnp.broadcast_to(steep[:, h : h + 1], (size, LANES))


def weighted(h, planes, table, rise, ratio, mask):
    size = rise.shape[1]
    steep = rise[h].reshape(size // 16, 16, LANES)
    left = jnp.concatenate([table[h, t] for t in range(size // LANES)], axis=1)
    cols = []
    for plane in planes:
        w = jnp.maximum(steep, ratio[h, plane][None]) * mask[plane].reshape(size // 16, 16, LANES)
        cols.append(w.reshape(size, LANES))
    return mm(left, jnp.concatenate(cols, axis=1))


def elu(x):
    small = x * (1.0 + 0.5 * x)
    low = jnp.where(x > -1e-3, small, jnp.exp(jnp.minimum(x, 0.0)) - 1.0)
    return jnp.where(x > 0, x, low)


def largest(*scores):
    worst = functools.reduce(jnp.maximum, [jnp.max(jnp.abs(s), axis=1, keepdims=True) for s in scores])
    return jnp.broadcast_to(worst, (HEADS, LANES))


def turned_tile(m, diagonal):
    m = m.astype(F32)
    if diagonal is not None:
        m = jnp.where(iota(m.shape, 0) == iota(m.shape, 1) + diagonal, 1.0, m)
    return m.astype(BF16).T


def turn_kernel(count_ref, edge_hbm, bound_hbm, edge_out, bound_out, edge, bound, edge_t, bound_t, sems, sent):
    nodes, slots = bound.shape
    hops = edge.shape[0]
    half = nodes // 2
    planes = nodes // LANES
    cap = slots // count_ref.shape[0]
    parts = [(hop, i) for hop in range(hops) for i in range(2)]
    copies, sends = [], []
    for k, (hop, i) in enumerate(parts):
        rows, some = pl.ds(i * half, half), pl.ds(i * planes // 2, planes // 2)
        copies.append(pltpu.make_async_copy(edge_hbm.at[hop, rows, :], edge.at[hop, rows, :], sems.at[k]))
        sends.append(pltpu.make_async_copy(edge_t.at[hop, some], edge_out.at[hop, some], sent.at[k]))
    copies.append(pltpu.make_async_copy(bound_hbm, bound, sems.at[2 * hops]))
    sends.append(pltpu.make_async_copy(bound_t, bound_out, sent.at[2 * hops]))
    for copy in copies:
        copy.start()
    lane = iota((1, slots), 1)
    live = jnp.zeros((1, slots), F32)
    for p in range(count_ref.shape[0]):
        live = jnp.where((lane // cap == p) & (lane % cap < count_ref[p]), 1.0, live)
    for k, (hop, i) in enumerate(parts):
        copies[k].wait()
        for plane in range(i * planes // 2, (i + 1) * planes // 2):
            rows = slice(plane * LANES, (plane + 1) * LANES)
            for t in range(planes):
                lanes = slice(t * LANES, (t + 1) * LANES)
                edge_t[hop, plane, lanes, :] = turned_tile(edge[hop, rows, lanes], 0 if hop == 0 and t == plane else None)
        sends[k].start()
    copies[2 * hops].wait()
    for plane in range(planes):
        m = bound[plane * LANES : (plane + 1) * LANES, :].astype(F32) * live
        for t in range(slots // LANES):
            lanes = slice(t * LANES, (t + 1) * LANES)
            bound_t[plane, lanes, :] = turned_tile(m[:, lanes], None)
    sends[2 * hops].start()
    for send in sends:
        send.wait()


def turn_masks(counts, edges, bound):
    hops, nodes = EARLY, edges.shape[1]
    slots = bound.shape[1]
    planes = nodes // LANES
    far = pl.BlockSpec(memory_space=pl.ANY)
    edge_t, bound_t = pl.pallas_call(
        turn_kernel,
        out_shape=(
            jax.ShapeDtypeStruct((hops, planes, nodes, LANES), BF16),
            jax.ShapeDtypeStruct((planes, slots, LANES), BF16),
        ),
        in_specs=[pl.BlockSpec(memory_space=pltpu.SMEM), far, far],
        out_specs=(pl.BlockSpec(memory_space=pltpu.HBM),) * 2,
        scratch_shapes=[
            pltpu.VMEM((hops, nodes, nodes), jnp.int32),
            pltpu.VMEM((nodes, slots), jnp.int32),
            pltpu.VMEM((hops, planes, nodes, LANES), BF16),
            pltpu.VMEM((planes, slots, LANES), BF16),
            pltpu.SemaphoreType.DMA((2 * hops + 1,)),
            pltpu.SemaphoreType.DMA((2 * hops + 1,)),
        ],
        compiler_params=pltpu.CompilerParams(vmem_limit_bytes=58 << 20),
        name="turn_masks",
    )(counts, in_hbm(edges), in_hbm(bound))
    return in_hbm(edge_t), in_hbm(bound_t)


def scratch(size, nodes, copies):
    planes = nodes // LANES
    return (
        *[pltpu.VMEM((HEADS, size // LANES, ROWS, LANES), BF16)] * copies,
        *[pltpu.VMEM((HEADS, size, LANES), BF16)] * copies,
        *[pltpu.VMEM((planes, size, LANES), BF16)] * copies,
        pltpu.VMEM((HEADS, planes, 16, LANES), BF16),
    )


def spread_ratio(d, ratio):
    r = jnp.exp(-0.8 * d)
    for h in range(HEADS):
        for p in range(d.shape[1] // LANES):
            row = r[h : h + 1, p * LANES : (p + 1) * LANES]
            ratio[h, p] = jnp.broadcast_to(row, (16, LANES)).astype(BF16)


def blocks_kernel(
    x0, x1, x2, x3, x4, proj_ref, src_ref, dst_ref, mask_hbm, edge_hbm,
    acc_ref, dst_out, worst_ref, landed, raw, sems
):
    nodes = x0.shape[0]
    planes = nodes // LANES
    per = TILE // LANES
    xs = (x0, x1, x2, x3, x4)
    copies = [pltpu.make_async_copy(mask_hbm.at[b], landed.at[b], sems.at[b]) for b in range(EARLY)]
    for b in range(EARLY, HOPS):
        copies.append(pltpu.make_async_copy(edge_hbm.at[b], raw.at[b - EARLY], sems.at[b]))
    tiles = [(plane, t) for plane in range(planes) for t in range(planes)]
    share = -(-len(tiles) // HEADS)
    for copy in copies:
        copy.start()

    def body(table_a, table_b, rise_a, rise_b, mask_a, mask_b, ratio):
        tables, rises, masks = (table_a, table_b), (rise_a, rise_b), (mask_a, mask_b)
        proj_t = proj_ref[...].T
        spread = spread_heads(src_ref[...])

        def begin(b):
            turned = mm(proj_t, xs[b][...], NT).astype(BF16)
            return turned, logits(spread, turned)

        turned, s = begin(0)
        d = logits(spread_heads(dst_ref[...]), turned)
        dst_out[...] = d
        spread_ratio(d, ratio)
        worst = largest(s, d)
        flat, steep = steps(s)
        for h in range(HEADS):
            prepare(h, turned, flat, steep, table_a, rise_a)
        copies[0].wait()
        for p in range(planes):
            mask_a[p] = landed[0, p]
        for b in range(HOPS):
            now, later = b % 2, (b + 1) % 2
            if b + 1 < HOPS:
                turned, s = begin(b + 1)
                worst = jnp.maximum(worst, largest(s))
                flat, steep = steps(s)
                copies[b + 1].wait()
                if b + 1 < EARLY:
                    for p in range(planes):
                        masks[later][p] = landed[b + 1, p]
            for h in range(HEADS):
                if b + 1 < HOPS:
                    prepare(h, turned, flat, steep, tables[later], rises[later])
                    if b + 1 >= EARLY:
                        for plane, t in tiles[h * share : (h + 1) * share]:
                            cut = slice(t * LANES, (t + 1) * LANES)
                            tile = raw[b + 1 - EARLY, plane * LANES : (plane + 1) * LANES, cut]
                            masks[later][plane, cut, :] = turned_tile(tile, None)
                for i in range(nodes // TILE):
                    lanes = slice(i * TILE, (i + 1) * TILE)
                    part = weighted(h, range(i * per, (i + 1) * per), tables[now], rises[now], ratio, masks[now])
                    acc_ref[h, :, lanes] = part if b == 0 else acc_ref[h, :, lanes] + part
        worst_ref[...] = worst

    pl.run_scoped(body, *scratch(nodes, nodes, 2))


def node_blocks(blocks, proj, att_src, att_dst, mask, edges):
    nodes = blocks[0].shape[0]
    shape = jax.ShapeDtypeStruct
    return pl.pallas_call(
        blocks_kernel,
        out_shape=(shape((HEADS, ROWS, nodes), F32), shape((HEADS, nodes), F32), shape((HEADS, LANES), F32)),
        in_specs=[WHOLE] * 8 + [pl.BlockSpec(memory_space=pl.ANY)] * 2,
        out_specs=(WHOLE,) * 3,
        scratch_shapes=[
            pltpu.VMEM(mask.shape, BF16),
            pltpu.VMEM((HOPS - EARLY, nodes, nodes), jnp.int32),
            pltpu.SemaphoreType.DMA((HOPS,)),
        ],
        compiler_params=pltpu.CompilerParams(vmem_limit_bytes=30 << 20),
        name="node_blocks",
    )(*blocks, proj, att_src, att_dst, mask, in_hbm(edges))


def last_kernel(
    x0, x1, x2, x3, x4, xs, proj_ref, src_ref, dst_ref, worst_a, acc_in, slot_hbm, edge_any,
    out_ref,
    mask_ref, sem, turned_out, raw, hidden, cols, masks, tops, sums,
):
    nodes = x0.shape[0]
    planes = nodes // LANES
    per = TILE // LANES
    arrival = pltpu.make_async_copy(slot_hbm, mask_ref, sem)
    arrival.start()
    turned_slots = mm(proj_ref[...].T, xs[...], NT).astype(BF16)
    slot_scores = logits(spread_heads(src_ref[...]), turned_slots)
    worst = jnp.max(jnp.maximum(worst_a[...], largest(slot_scores)))
    arrival.wait()

    def finish(h, acc):
        o = acc[0:HEAD_DIM] * (1.0 / acc[HEAD_DIM : HEAD_DIM + 1])
        turned_out[h * HEAD_DIM : (h + 1) * HEAD_DIM, :] = elu(o)

    @pl.when(worst <= SPAN)
    def _():
        def body(table, rise, mask, ratio):
            spread_ratio(dst_ref[...], ratio)
            flat, steep = steps(slot_scores)
            for p in range(planes):
                mask[p] = mask_ref[p]
            for h in range(HEADS):
                prepare(h, turned_slots, flat, steep, table, rise)
            for i in range(nodes // TILE):
                lanes = slice(i * TILE, (i + 1) * TILE)
                for h in range(HEADS):
                    part = weighted(h, range(i * per, (i + 1) * per), table, rise, ratio, mask)
                    finish(h, acc_in[h, :, lanes] + part)
                out_ref[lanes, :] = turned_out[...].T.astype(BF16)

        pl.run_scoped(body, *scratch(xs.shape[0], nodes, 1))

    @pl.when(jnp.logical_not(worst <= SPAN))
    def _():
        tops[...] = jnp.full(tops.shape, -jnp.inf, F32)
        sums[...] = jnp.zeros(sums.shape, F32)
        for second in (False, True):
            for b, x in enumerate((x0, x1, x2, x3, x4, xs)):
                size = x.shape[0]
                if b == HOPS:
                    masks[:, 0:size, :] = mask_ref[...]
                else:

                    def turn(p, carry):
                        pltpu.sync_copy(edge_any.at[b, pl.ds(pl.multiple_of(p * LANES, LANES), LANES), :], raw)
                        for t in range(planes):
                            lanes = slice(t * LANES, (t + 1) * LANES)
                            diagonal = (t - p) * LANES if b == 0 else None
                            masks[p, lanes, :] = turned_tile(raw[:, lanes], diagonal)
                        return carry

                    lax.fori_loop(0, planes, turn, 0)
                turned = mm(proj_ref[...].T, x[...], NT).astype(BF16)
                cols[0:size] = logits(spread_heads(src_ref[...]), turned).T
                for h in range(HEADS):
                    hidden[h, 0:HEAD_DIM, 0:size] = turned[h * HEAD_DIM : (h + 1) * HEAD_DIM]
                    hidden[h, HEAD_DIM:ROWS, 0:size] = jnp.ones((ROWS - HEAD_DIM, size), BF16)

                def one(i, carry):
                    h, p = i // planes, i % planes
                    lanes = pl.ds(pl.multiple_of(p * LANES, LANES), LANES)
                    c = cols[0:size]
                    s = jnp.sum(jnp.where(iota(c.shape, 1) == h, c, 0.0), axis=1, keepdims=True)
                    d = dst_ref[:, lanes]
                    v = s + jnp.sum(jnp.where(iota(d.shape, 0) == h, d, 0.0), axis=0, keepdims=True)
                    v = jnp.maximum(v, 0.2 * v)
                    v = jnp.where(masks[p, 0:size].astype(F32) > 0, v, -jnp.inf)
                    if second:
                        w = jnp.exp(v - tops[h, 0:1, lanes]).astype(BF16)
                        sums[h, :, lanes] += mm(hidden[h, :, 0:size], w)
                    else:
                        tops[h, :, lanes] = jnp.maximum(tops[h, :, lanes], jnp.max(v, axis=0, keepdims=True))
                    return carry

                lax.fori_loop(0, HEADS * planes, one, 0)
        for i in range(nodes // TILE):
            lanes = slice(i * TILE, (i + 1) * TILE)
            for h in range(HEADS):
                finish(h, sums[h, :, lanes])
            out_ref[lanes, :] = turned_out[...].T.astype(BF16)


def last_block(blocks, slots, proj, att_src, dst, worst, acc, bound, edges):
    nodes = acc.shape[2]
    width = proj.shape[1]
    return pl.pallas_call(
        last_kernel,
        out_shape=jax.ShapeDtypeStruct((nodes, width), BF16),
        in_specs=[WHOLE] * 11 + [pl.BlockSpec(memory_space=pl.ANY)] * 2,
        out_specs=WHOLE,
        scratch_shapes=[
            pltpu.VMEM(bound.shape, BF16),
            pltpu.SemaphoreType.DMA,
            pltpu.VMEM((width, TILE), F32),
            pltpu.VMEM((LANES, nodes), jnp.int32),
            pltpu.VMEM((HEADS, ROWS, nodes), BF16),
            pltpu.VMEM((nodes, HEADS), F32),
            pltpu.VMEM((nodes // LANES, nodes, LANES), BF16),
            pltpu.VMEM((HEADS, 8, nodes), F32),
            pltpu.VMEM((HEADS, ROWS, nodes), F32),
        ],
        compiler_params=pltpu.CompilerParams(vmem_limit_bytes=24 << 20),
        name="last_block",
    )(*blocks, slots, proj, att_src, dst, worst, acc, bound, edges)


def attend(counts, blocks, slots, proj, att_src, att_dst, edges, bound):
    mask, bound = turn_masks(counts, edges, bound)
    acc, dst, worst = node_blocks(blocks, proj, att_src, att_dst, mask, edges)
    return last_block(blocks, slots, proj, att_src, dst, worst, acc, bound, in_hbm(edges))


def passed_along(block, axis, distance):
    devices = range(lax.axis_size(axis))
    return lax.ppermute(block, axis, [((i - distance) % len(devices), i) for i in devices])


def other_core(block):
    return lax.ppermute(block, "blk", [(i, i ^ 1) for i in range(lax.axis_size("blk"))])


def local(feats, proj, att_src, att_dst, edge_mask, send_rows, send_count, bound_mask):
    edges = in_hbm(jnp.transpose(edge_mask, (1, 0, 2)))
    two = passed_along(feats, "blk", 2)
    four = passed_along(feats, "blk", 4)
    outgoing = pick_rows(send_rows[0], feats)
    arrived = lax.all_to_all(outgoing, "grp", split_axis=0, concat_axis=0, tiled=True)
    mask, bound = turn_masks(in_hbm(send_count.reshape(-1)), edges, bound_mask)
    two, four, mask, _ = lax.optimization_barrier((two, four, mask, outgoing))
    mask = in_hbm(mask)
    second = lax.axis_index("blk") % 2 == 1
    outer = other_core(jnp.where(second, four, feats))
    inner = other_core(two)
    one = jnp.where(second, outer, inner)
    three = jnp.where(second, inner, outer)
    blocks = (feats, one, two, three, four)
    acc, dst, worst = node_blocks(blocks, proj, att_src, att_dst, mask, edges)
    return last_block(blocks, arrived, proj, att_src, dst, worst, acc, bound, edges)


def solution(mesh):
    in_specs = (
        P(("grp", "blk"), None),
        P(),
        P(),
        P(),
        P(("grp", "blk"), None, None),
        P(("grp", "blk"), None, None),
        P(None, "blk", "grp"),
        P(("grp", "blk"), None),
    )
    out_specs = P(("grp", "blk"), None)
    return jax.shard_map(local, mesh=mesh, in_specs=in_specs, out_specs=out_specs, check_vma=False)
```

```python
import functools

import jax
import jax.numpy as jnp
from jax import lax
from jax.experimental import pallas as pl
from jax.experimental.pallas import tpu as pltpu
from jax.sharding import PartitionSpec as P

HEADS = 8
HEAD_DIM = 64
HOPS = 5
LANES = 128
ROWS = 80
TILE = 256
EARLY = 3
SPAN = 60.0
F32 = jnp.float32
BF16 = jnp.bfloat16
NT = (((1,), (1,)), ((), ()))
NN = (((1,), (0,)), ((), ()))
WHOLE = pl.BlockSpec(memory_space=pltpu.VMEM)


def mm(a, b, dims=NN):
    return lax.dot_general(a, b, dims, preferred_element_type=F32)


def in_hbm(x):
    return pltpu.with_memory_space_constraint(x, pltpu.HBM)


def iota(shape, axis):
    return lax.broadcasted_iota(jnp.int32, shape, axis)


def pieces(x):
    hi = x.astype(BF16)
    rest = x - hi.astype(F32)
    mid = rest.astype(BF16)
    low = (rest - mid.astype(F32)).astype(BF16)
    return hi, mid, low


def pick_kernel(rows_ref, feats_ref, out_ref, chosen):
    groups, cap = rows_ref.shape
    count = feats_ref.shape[0]
    rows = rows_ref[...].astype(F32)
    high = jnp.floor(rows * (1.0 / 256.0))
    low = rows - 256.0 * high
    unit = jnp.where(iota((cap, cap), 0) == iota((cap, cap), 1), 1.0, 0.0).astype(BF16)
    turned = mm(unit, high.astype(BF16), NT) * 256.0 + mm(unit, low.astype(BF16), NT)
    turned = turned.astype(jnp.int32)
    lane = iota((cap, count), 1)
    for p in range(groups):
        hit = lane == turned[:, p : p + 1]
        chosen[p * cap : (p + 1) * cap, :] = jnp.where(hit, 1.0, 0.0).astype(BF16)
    out_ref[...] = mm(chosen[...], feats_ref[...]).astype(BF16)


def pick_rows(send_rows, feats):
    groups, cap = send_rows.shape
    return pl.pallas_call(
        pick_kernel,
        out_shape=jax.ShapeDtypeStruct((groups * cap, feats.shape[1]), BF16),
        scratch_shapes=[pltpu.VMEM((groups * cap, feats.shape[0]), BF16)],
        name="pick_rows",
    )(send_rows, feats)


def spread_heads(vector):
    width = HEADS * HEAD_DIM
    tiler = jnp.where(iota((HEAD_DIM, width), 1) % HEAD_DIM == iota((HEAD_DIM, width), 0), 1.0, 0.0).astype(BF16)
    own = iota((HEADS, width), 1) // HEAD_DIM == iota((HEADS, width), 0)
    parts = [jnp.where(own, mm(p, tiler), 0.0) for p in pieces(vector)]
    parts.append(jnp.zeros((HEADS, width), F32))
    return jnp.concatenate(parts, axis=0).astype(BF16)


def logits(spread, turned):
    s = mm(spread, turned)
    return s[0:HEADS] + s[HEADS : 2 * HEADS] + s[2 * HEADS : 3 * HEADS]


def steps(s):
    return jnp.exp(0.2 * s), jnp.exp(0.8 * s).T.astype(BF16)


def prepare(h, turned, flat, steep, table, rise):
    size = flat.shape[1]
    tail = jnp.broadcast_to(flat[h : h + 1], (ROWS - HEAD_DIM, size)).astype(BF16)
    part = turned[h * HEAD_DIM : (h + 1) * HEAD_DIM].reshape(HEAD_DIM // 16, 16, size) * tail[None]
    part = part.reshape(HEAD_DIM, size)
    for t in range(size // LANES):
        lanes = slice(t * LANES, (t + 1) * LANES)
        table[h, t, 0:HEAD_DIM, :] = part[:, lanes]
        table[h, t, HEAD_DIM:ROWS, :] = tail[:, lanes]
    rise[h] = jnp.broadcast_to(steep[:, h : h + 1], (size, LANES))


def weighted(h, planes, table, rise, ratio, mask):
    size = rise.shape[1]
    steep = rise[h].reshape(size // 16, 16, LANES)
    left = jnp.concatenate([table[h, t] for t in range(size // LANES)], axis=1)
    cols = []
    for plane in planes:
        w = jnp.maximum(steep, ratio[h, plane][None]) * mask[plane].reshape(size // 16, 16, LANES)
        cols.append(w.reshape(size, LANES))
    return mm(left, jnp.concatenate(cols, axis=1))


def elu(x):
    small = x * (1.0 + 0.5 * x)
    low = jnp.where(x > -1e-3, small, jnp.exp(jnp.minimum(x, 0.0)) - 1.0)
    return jnp.where(x > 0, x, low)


def largest(*scores):
    worst = functools.reduce(jnp.maximum, [jnp.max(jnp.abs(s), axis=1, keepdims=True) for s in scores])
    return jnp.broadcast_to(worst, (HEADS, LANES))


def turned_tile(m, diagonal):
    m = m.astype(F32)
    if diagonal is not None:
        m = jnp.where(iota(m.shape, 0) == iota(m.shape, 1) + diagonal, 1.0, m)
    return m.astype(BF16).T


def turn_kernel(count_ref, edge_hbm, bound_hbm, edge_out, bound_out, edge, bound, edge_t, bound_t, sems, sent):
    nodes, slots = bound.shape
    hops = edge.shape[0]
    half = nodes // 2
    planes = nodes // LANES
    cap = slots // count_ref.shape[0]
    parts = [(hop, i) for hop in range(hops) for i in range(2)]
    copies, sends = [], []
    for k, (hop, i) in enumerate(parts):
        rows, some = pl.ds(i * half, half), pl.ds(i * planes // 2, planes // 2)
        copies.append(pltpu.make_async_copy(edge_hbm.at[hop, rows, :], edge.at[hop, rows, :], sems.at[k]))
        sends.append(pltpu.make_async_copy(edge_t.at[hop, some], edge_out.at[hop, some], sent.at[k]))
    copies.append(pltpu.make_async_copy(bound_hbm, bound, sems.at[2 * hops]))
    sends.append(pltpu.make_async_copy(bound_t, bound_out, sent.at[2 * hops]))
    for copy in copies:
        copy.start()
    lane = iota((1, slots), 1)
    live = jnp.zeros((1, slots), F32)
    for p in range(count_ref.shape[0]):
        live = jnp.where((lane // cap == p) & (lane % cap < count_ref[p]), 1.0, live)
    for k, (hop, i) in enumerate(parts):
        copies[k].wait()
        for plane in range(i * planes // 2, (i + 1) * planes // 2):
            rows = slice(plane * LANES, (plane + 1) * LANES)
            for t in range(planes):
                lanes = slice(t * LANES, (t + 1) * LANES)
                edge_t[hop, plane, lanes, :] = turned_tile(edge[hop, rows, lanes], 0 if hop == 0 and t == plane else None)
        sends[k].start()
    copies[2 * hops].wait()
    for plane in range(planes):
        m = bound[plane * LANES : (plane + 1) * LANES, :].astype(F32) * live
        for t in range(slots // LANES):
            lanes = slice(t * LANES, (t + 1) * LANES)
            bound_t[plane, lanes, :] = turned_tile(m[:, lanes], None)
    sends[2 * hops].start()
    for send in sends:
        send.wait()


def turn_masks(counts, edges, bound):
    hops, nodes = EARLY, edges.shape[1]
    slots = bound.shape[1]
    planes = nodes // LANES
    far = pl.BlockSpec(memory_space=pl.ANY)
    edge_t, bound_t = pl.pallas_call(
        turn_kernel,
        out_shape=(
            jax.ShapeDtypeStruct((hops, planes, nodes, LANES), BF16),
            jax.ShapeDtypeStruct((planes, slots, LANES), BF16),
        ),
        in_specs=[pl.BlockSpec(memory_space=pltpu.SMEM), far, far],
        out_specs=(pl.BlockSpec(memory_space=pltpu.HBM),) * 2,
        scratch_shapes=[
            pltpu.VMEM((hops, nodes, nodes), jnp.int32),
            pltpu.VMEM((nodes, slots), jnp.int32),
            pltpu.VMEM((hops, planes, nodes, LANES), BF16),
            pltpu.VMEM((planes, slots, LANES), BF16),
            pltpu.SemaphoreType.DMA((2 * hops + 1,)),
            pltpu.SemaphoreType.DMA((2 * hops + 1,)),
        ],
        compiler_params=pltpu.CompilerParams(vmem_limit_bytes=58 << 20),
        name="turn_masks",
    )(counts, in_hbm(edges), in_hbm(bound))
    return in_hbm(edge_t), in_hbm(bound_t)


def scratch(size, nodes, copies):
    planes = nodes // LANES
    return (
        *[pltpu.VMEM((HEADS, size // LANES, ROWS, LANES), BF16)] * copies,
        *[pltpu.VMEM((HEADS, size, LANES), BF16)] * copies,
        *[pltpu.VMEM((planes, size, LANES), BF16)] * copies,
        pltpu.VMEM((HEADS, planes, 16, LANES), BF16),
    )


def spread_ratio(d, ratio):
    r = jnp.exp(-0.8 * d)
    for h in range(HEADS):
        for p in range(d.shape[1] // LANES):
            row = r[h : h + 1, p * LANES : (p + 1) * LANES]
            ratio[h, p] = jnp.broadcast_to(row, (16, LANES)).astype(BF16)


def blocks_kernel(
    x0, x1, x2, x3, x4, proj_ref, src_ref, dst_ref, mask_hbm, edge_hbm,
    acc_ref, dst_out, worst_ref, landed, raw, sems
):
    nodes = x0.shape[0]
    planes = nodes // LANES
    per = TILE // LANES
    xs = (x0, x1, x2, x3, x4)
    copies = [pltpu.make_async_copy(mask_hbm.at[b], landed.at[b], sems.at[b]) for b in range(EARLY)]
    for b in range(EARLY, HOPS):
        copies.append(pltpu.make_async_copy(edge_hbm.at[b], raw.at[b - EARLY], sems.at[b]))
    tiles = [(plane, t) for plane in range(planes) for t in range(planes)]
    share = -(-len(tiles) // HEADS)
    for copy in copies:
        copy.start()

    def body(table_a, table_b, rise_a, rise_b, mask_a, mask_b, ratio):
        tables, rises, masks = (table_a, table_b), (rise_a, rise_b), (mask_a, mask_b)
        proj_t = proj_ref[...].T
        spread = spread_heads(src_ref[...])

        def begin(b):
            turned = mm(proj_t, xs[b][...], NT).astype(BF16)
            return turned, logits(spread, turned)

        turned, s = begin(0)
        d = logits(spread_heads(dst_ref[...]), turned)
        dst_out[...] = d
        spread_ratio(d, ratio)
        worst = largest(s, d)
        flat, steep = steps(s)
        for h in range(HEADS):
            prepare(h, turned, flat, steep, table_a, rise_a)
        copies[0].wait()
        for p in range(planes):
            mask_a[p] = landed[0, p]
        for b in range(HOPS):
            now, later = b % 2, (b + 1) % 2
            if b + 1 < HOPS:
                turned, s = begin(b + 1)
                worst = jnp.maximum(worst, largest(s))
                flat, steep = steps(s)
                copies[b + 1].wait()
                if b + 1 < EARLY:
                    for p in range(planes):
                        masks[later][p] = landed[b + 1, p]
            for h in range(HEADS):
                if b + 1 < HOPS:
                    prepare(h, turned, flat, steep, tables[later], rises[later])
                    if b + 1 >= EARLY:
                        for plane, t in tiles[h * share : (h + 1) * share]:
                            cut = slice(t * LANES, (t + 1) * LANES)
                            tile = raw[b + 1 - EARLY, plane * LANES : (plane + 1) * LANES, cut]
                            masks[later][plane, cut, :] = turned_tile(tile, None)
                for i in range(nodes // TILE):
                    lanes = slice(i * TILE, (i + 1) * TILE)
                    part = weighted(h, range(i * per, (i + 1) * per), tables[now], rises[now], ratio, masks[now])
                    acc_ref[h, :, lanes] = part if b == 0 else acc_ref[h, :, lanes] + part
        worst_ref[...] = worst

    pl.run_scoped(body, *scratch(nodes, nodes, 2))


def node_blocks(blocks, proj, att_src, att_dst, mask, edges):
    nodes = blocks[0].shape[0]
    shape = jax.ShapeDtypeStruct
    return pl.pallas_call(
        blocks_kernel,
        out_shape=(shape((HEADS, ROWS, nodes), F32), shape((HEADS, nodes), F32), shape((HEADS, LANES), F32)),
        in_specs=[WHOLE] * 8 + [pl.BlockSpec(memory_space=pl.ANY)] * 2,
        out_specs=(WHOLE,) * 3,
        scratch_shapes=[
            pltpu.VMEM(mask.shape, BF16),
            pltpu.VMEM((HOPS - EARLY, nodes, nodes), jnp.int32),
            pltpu.SemaphoreType.DMA((HOPS,)),
        ],
        compiler_params=pltpu.CompilerParams(vmem_limit_bytes=30 << 20),
        name="node_blocks",
    )(*blocks, proj, att_src, att_dst, mask, in_hbm(edges))


def last_kernel(
    x0, x1, x2, x3, x4, xs, proj_ref, src_ref, dst_ref, worst_a, acc_in, slot_hbm, edge_any,
    out_ref,
    mask_ref, sem, turned_out, raw, hidden, cols, masks, tops, sums,
):
    nodes = x0.shape[0]
    planes = nodes // LANES
    per = TILE // LANES
    arrival = pltpu.make_async_copy(slot_hbm, mask_ref, sem)
    arrival.start()
    turned_slots = mm(proj_ref[...].T, xs[...], NT).astype(BF16)
    slot_scores = logits(spread_heads(src_ref[...]), turned_slots)
    worst = jnp.max(jnp.maximum(worst_a[...], largest(slot_scores)))
    arrival.wait()

    def finish(h, acc):
        o = acc[0:HEAD_DIM] * (1.0 / acc[HEAD_DIM : HEAD_DIM + 1])
        turned_out[h * HEAD_DIM : (h + 1) * HEAD_DIM, :] = elu(o).astype(BF16)

    @pl.when(worst <= SPAN)
    def _():
        def body(table, rise, mask, ratio):
            spread_ratio(dst_ref[...], ratio)
            flat, steep = steps(slot_scores)
            for p in range(planes):
                mask[p] = mask_ref[p]
            for h in range(HEADS):
                prepare(h, turned_slots, flat, steep, table, rise)
            for i in range(nodes // TILE):
                lanes = slice(i * TILE, (i + 1) * TILE)
                for h in range(HEADS):
                    part = weighted(h, range(i * per, (i + 1) * per), table, rise, ratio, mask)
                    finish(h, acc_in[h, :, lanes] + part)
                out_ref[lanes, :] = turned_out[...].T

        pl.run_scoped(body, *scratch(xs.shape[0], nodes, 1))

    @pl.when(jnp.logical_not(worst <= SPAN))
    def _():
        tops[...] = jnp.full(tops.shape, -jnp.inf, F32)
        sums[...] = jnp.zeros(sums.shape, F32)
        for second in (False, True):
            for b, x in enumerate((x0, x1, x2, x3, x4, xs)):
                size = x.shape[0]
                if b == HOPS:
                    masks[:, 0:size, :] = mask_ref[...]
                else:

                    def turn(p, carry):
                        pltpu.sync_copy(edge_any.at[b, pl.ds(pl.multiple_of(p * LANES, LANES), LANES), :], raw)
                        for t in range(planes):
                            lanes = slice(t * LANES, (t + 1) * LANES)
                            diagonal = (t - p) * LANES if b == 0 else None
                            masks[p, lanes, :] = turned_tile(raw[:, lanes], diagonal)
                        return carry

                    lax.fori_loop(0, planes, turn, 0)
                turned = mm(proj_ref[...].T, x[...], NT).astype(BF16)
                cols[0:size] = logits(spread_heads(src_ref[...]), turned).T
                for h in range(HEADS):
                    hidden[h, 0:HEAD_DIM, 0:size] = turned[h * HEAD_DIM : (h + 1) * HEAD_DIM]
                    hidden[h, HEAD_DIM:ROWS, 0:size] = jnp.ones((ROWS - HEAD_DIM, size), BF16)

                def one(i, carry):
                    h, p = i // planes, i % planes
                    lanes = pl.ds(pl.multiple_of(p * LANES, LANES), LANES)
                    c = cols[0:size]
                    s = jnp.sum(jnp.where(iota(c.shape, 1) == h, c, 0.0), axis=1, keepdims=True)
                    d = dst_ref[:, lanes]
                    v = s + jnp.sum(jnp.where(iota(d.shape, 0) == h, d, 0.0), axis=0, keepdims=True)
                    v = jnp.maximum(v, 0.2 * v)
                    v = jnp.where(masks[p, 0:size].astype(F32) > 0, v, -jnp.inf)
                    if second:
                        w = jnp.exp(v - tops[h, 0:1, lanes]).astype(BF16)
                        sums[h, :, lanes] += mm(hidden[h, :, 0:size], w)
                    else:
                        tops[h, :, lanes] = jnp.maximum(tops[h, :, lanes], jnp.max(v, axis=0, keepdims=True))
                    return carry

                lax.fori_loop(0, HEADS * planes, one, 0)
        for i in range(nodes // TILE):
            lanes = slice(i * TILE, (i + 1) * TILE)
            for h in range(HEADS):
                finish(h, sums[h, :, lanes])
            out_ref[lanes, :] = turned_out[...].T


def last_block(blocks, slots, proj, att_src, dst, worst, acc, bound, edges):
    nodes = acc.shape[2]
    width = proj.shape[1]
    return pl.pallas_call(
        last_kernel,
        out_shape=jax.ShapeDtypeStruct((nodes, width), BF16),
        in_specs=[WHOLE] * 11 + [pl.BlockSpec(memory_space=pl.ANY)] * 2,
        out_specs=WHOLE,
        scratch_shapes=[
            pltpu.VMEM(bound.shape, BF16),
            pltpu.SemaphoreType.DMA,
            pltpu.VMEM((width, TILE), BF16),
            pltpu.VMEM((LANES, nodes), jnp.int32),
            pltpu.VMEM((HEADS, ROWS, nodes), BF16),
            pltpu.VMEM((nodes, HEADS), F32),
            pltpu.VMEM((nodes // LANES, nodes, LANES), BF16),
            pltpu.VMEM((HEADS, 8, nodes), F32),
            pltpu.VMEM((HEADS, ROWS, nodes), F32),
        ],
        compiler_params=pltpu.CompilerParams(vmem_limit_bytes=24 << 20),
        name="last_block",
    )(*blocks, slots, proj, att_src, dst, worst, acc, bound, edges)


def attend(counts, blocks, slots, proj, att_src, att_dst, edges, bound):
    mask, bound = turn_masks(counts, edges, bound)
    acc, dst, worst = node_blocks(blocks, proj, att_src, att_dst, mask, edges)
    return last_block(blocks, slots, proj, att_src, dst, worst, acc, bound, in_hbm(edges))


def passed_along(block, axis, distance):
    devices = range(lax.axis_size(axis))
    return lax.ppermute(block, axis, [((i - distance) % len(devices), i) for i in devices])


def other_core(block):
    return lax.ppermute(block, "blk", [(i, i ^ 1) for i in range(lax.axis_size("blk"))])


def local(feats, proj, att_src, att_dst, edge_mask, send_rows, send_count, bound_mask):
    edges = in_hbm(jnp.transpose(edge_mask, (1, 0, 2)))
    two = passed_along(feats, "blk", 2)
    four = passed_along(feats, "blk", 4)
    outgoing = pick_rows(send_rows[0], feats)
    arrived = lax.all_to_all(outgoing, "grp", split_axis=0, concat_axis=0, tiled=True)
    mask, bound = turn_masks(in_hbm(send_count.reshape(-1)), edges, bound_mask)
    two, four, mask, _ = lax.optimization_barrier((two, four, mask, outgoing))
    mask = in_hbm(mask)
    second = lax.axis_index("blk") % 2 == 1
    outer = other_core(jnp.where(second, four, feats))
    inner = other_core(two)
    one = jnp.where(second, outer, inner)
    three = jnp.where(second, inner, outer)
    blocks = (feats, one, two, three, four)
    acc, dst, worst = node_blocks(blocks, proj, att_src, att_dst, mask, edges)
    return last_block(blocks, arrived, proj, att_src, dst, worst, acc, bound, edges)


def solution(mesh):
    in_specs = (
        P(("grp", "blk"), None),
        P(),
        P(),
        P(),
        P(("grp", "blk"), None, None),
        P(("grp", "blk"), None, None),
        P(None, "blk", "grp"),
        P(("grp", "blk"), None),
    )
    out_specs = P(("grp", "blk"), None)
    return jax.shard_map(local, mesh=mesh, in_specs=in_specs, out_specs=out_specs, check_vma=False)
```
